256 devices in a mesh: ctx: 32 (over x_lo, z, core), head: 8 (over x_hi, y).
Axes of the slice: x: 4 (x_hi: 2, x_lo: 2; x = x_hi * 2 + x_lo), y: 4, z: 8, core: 2. Of those that a mesh axis runs over, the one named last changes fastest.
Arguments:
- queries: bfloat16 [16384, 16, 128], P('ctx', 'head'), may hold values from -40 to 40
- keys: bfloat16 [16384, 128], P('ctx'), may hold values from -5 to 5
- values: bfloat16 [16384, 128], P('ctx'), may hold values from -1.5 to 1.5
- grad_out: bfloat16 [16384, 16, 128], P('ctx', 'head'), may hold values from -6 to 6
- lengths: int32 [16], replicated, may hold values from 1 to 2048, 16384 in all
- tile_of: int32 [32], replicated, may hold values from 0 to 31, each once
Outputs:
- attended: bfloat16 [16384, 16, 128], P('ctx', 'head')
- grad_queries: bfloat16 [16384, 16, 128], P('ctx', 'head')
- grad_keys: float32 [16384, 128], P('ctx')
- grad_values: float32 [16384, 128], P('ctx')
The draws below stay inside these ranges and needn't reach their ends.
Inputs may be any that keep to these rules, and one draw needn't show every extreme that they name: 16 positive lengths summing to 16384; the longest is exactly 2048. `tile_of`: each tile number appears once.
All inputs are finite; a program needn't handle non-finite values.
Results may differ from the reference program's by a relative error of at most 0.025.
Values may be sent and summed in bfloat16 or wider, within the bound.
A program may use at most 128 MiB of HBM per device.

```python
import math
import jax
import jax.numpy as jnp
import numpy as np
from jax import lax

DH = 128
HQ = 16
TOK_DEV = 512
NDOCS = 16
TOKENS = 16384
MOST_DOC = 2048
N_CTX = 32


def draw_keys(key, part):
    result = jnp.clip(jax.random.normal(jax.random.fold_in(key, 13), (TOKENS, DH), jnp.float32), -4.0, 4.0)
    return result.astype(jnp.bfloat16)


def draw_queries(key, part):
    result = jnp.clip(jax.random.normal(jax.random.fold_in(key, 15), (TOKENS, HQ, DH), jnp.float32), -4.0, 4.0)
    return result.astype(jnp.bfloat16)


def steps_of(own_key, shape, pieces, smallest, top_value):
    def one(dim, blocks):
        heights = jax.random.uniform(jax.random.fold_in(jax.random.fold_in(own_key, 6), dim), (blocks,), jnp.float32, smallest / len(pieces), top_value / len(pieces))
        return jnp.repeat(jnp.exp(heights), shape[dim] // blocks).reshape((-1,) + (1,) * (len(shape) - dim - 1))

    level = one(*pieces[0])
    for cut in pieces[1:]:
        level = level * one(*cut)
    return level


def profile(amount, total, limit, lean):
    portions = [(1 << 20) // math.isqrt(rank ** lean) + 1 for rank in range(2, amount + 1)]
    spare, holding = total - limit - (amount - 1), [1] * (amount - 1)
    while spare > 0:
        movable = [i for i in range(amount - 1) if holding[i] < limit]
        mass, remaining = sum([portions[i] for i in movable]), spare
        for i in movable:
            addition = min(limit - holding[i], max(1, remaining * portions[i] // mass), spare)
            holding[i] = holding[i] + addition
            spare = spare - addition
    return np.array([limit] + holding)


def ragged(rng, number_of, total, reach, skew):
    if number_of == 2:
        one = jax.random.randint(rng, (), max(1, total - reach), min(reach, total - 1) + 1)
        return jnp.stack([one, total - one])
    sizes = jnp.asarray(profile(number_of, total, reach, skew), jnp.int32)
    couples = (number_of - 1) // 2
    source_of, taker = sizes[1:1 + 2 * couples:2], sizes[2:2 + 2 * couples:2]
    room = jnp.minimum(source_of - 1, reach - taker)
    shifted = jax.random.randint(jax.random.fold_in(rng, 1), (couples,), 0, 1 << 20) % (room + 1)
    sizes = sizes.at[1:1 + 2 * couples:2].set(source_of - shifted).at[2:2 + 2 * couples:2].set(taker + shifted)
    return sizes[jax.random.permutation(jax.random.fold_in(rng, 2), number_of)]


def bell_draw(stream_key, extent, deviation, reach, shards=(), held_as=jnp.bfloat16):
    factor_of = steps_of(stream_key, extent, shards, -0.22, 0.18) if shards else 1.0
    drawn = jax.random.normal(stream_key, extent, jnp.float32) * deviation * factor_of
    return jnp.minimum(jnp.maximum(drawn, -reach), reach).astype(held_as)


def setup_inputs(seed: int = 0) -> dict:
    arg_keys = jax.random.split(jax.random.key(seed), 7)
    queries = draw_queries(jax.random.fold_in(arg_keys[6], 71), 0)
    keys = draw_keys(jax.random.fold_in(arg_keys[6], 71), 0)
    values = bell_draw(arg_keys[2], (TOKENS, DH), 0.25, 1.5, ((0, 32),))
    grad_out = bell_draw(arg_keys[3], (TOKENS, HQ, DH), 1.0, 6.0, ((0, 32), (1, 8)))
    lengths = ragged(arg_keys[4], NDOCS, TOKENS, MOST_DOC, 2).astype(jnp.int32)
    tile_of = jax.random.permutation(arg_keys[5], N_CTX).astype(jnp.int32)
    return {"queries": queries, "keys": keys, "values": values, "grad_out": grad_out, "lengths": lengths, "tile_of": tile_of}


NEG_FILL = -1.0e30


def live_test(query_pos, query_doc, key_pos, key_doc):
    return (query_doc[:, None] == key_doc[None, :]) & (key_pos[None, :] <= query_pos[:, None])


def softmax_totals(query_rows, query_pos, query_doc, all_keys, key_pos, key_doc, key_block, score_scale):
    row_total = query_rows.shape[0]

    def loop_step(loop_index, carried):
        begin_row = (loop_index * key_block).astype(jnp.int32)
        key_rows = lax.dynamic_slice_in_dim(all_keys, begin_row, key_block, 0)
        block_pos = lax.dynamic_slice_in_dim(key_pos, begin_row, key_block, 0)
        block_doc = lax.dynamic_slice_in_dim(key_doc, begin_row, key_block, 0)
        live_mask = live_test(query_pos, query_doc, block_pos, block_doc)

        def update(state):
            running_max, running_sum = state
            scores = jnp.dot(query_rows, key_rows.T, preferred_element_type=jnp.float32) * score_scale
            scores = jnp.where(live_mask, scores, NEG_FILL)
            new_max = jnp.maximum(running_max, jnp.max(scores, axis=1))
            weights = jnp.where(live_mask, jnp.exp(scores - new_max[:, None]), 0.0)
            return new_max, running_sum * jnp.exp(running_max - new_max) + jnp.sum(weights, axis=1)

        return lax.cond(jnp.any(live_mask), update, lambda unchanged: unchanged, carried)

    start_state = (jnp.full((row_total,), NEG_FILL, jnp.float32), jnp.zeros((row_total,), jnp.float32))
    running_max, running_sum = lax.fori_loop(0, all_keys.shape[0] // key_block, loop_step, start_state)
    return running_max + jnp.log(running_sum)


def block_probs(query_rows, query_pos, query_doc, key_rows, block_pos, block_doc, log_total, score_scale):
    live_mask = live_test(query_pos, query_doc, block_pos, block_doc)
    scores = jnp.dot(query_rows, key_rows.T, preferred_element_type=jnp.float32) * score_scale
    return jnp.where(live_mask, jnp.exp(scores - log_total[:, None]), 0.0)


def attend_rows(query_rows, query_pos, query_doc, all_keys, all_values, key_pos, key_doc, key_block, log_total, score_scale):
    def loop_step(loop_index, accum):
        begin_row = (loop_index * key_block).astype(jnp.int32)
        key_rows = lax.dynamic_slice_in_dim(all_keys, begin_row, key_block, 0)
        value_rows = lax.dynamic_slice_in_dim(all_values, begin_row, key_block, 0)
        block_pos = lax.dynamic_slice_in_dim(key_pos, begin_row, key_block, 0)
        block_doc = lax.dynamic_slice_in_dim(key_doc, begin_row, key_block, 0)

        def update(total):
            probs = block_probs(query_rows, query_pos, query_doc, key_rows, block_pos, block_doc, log_total, score_scale)
            return total + jnp.dot(probs.astype(jnp.bfloat16), value_rows, preferred_element_type=jnp.float32)

        alive = jnp.any(live_test(query_pos, query_doc, block_pos, block_doc))
        return lax.cond(alive, update, lambda unchanged: unchanged, accum)

    start_total = jnp.zeros((query_rows.shape[0], all_values.shape[1]), jnp.float32)
    return lax.fori_loop(0, all_keys.shape[0] // key_block, loop_step, start_total)


def reference(queries, keys, values, grad_out, lengths, tile_of):
    score_scale = float(DH) ** -0.5
    offsets = jnp.arange(TOK_DEV, dtype=jnp.int32)
    positions = (tile_of[:, None].astype(jnp.int32) * TOK_DEV + offsets[None, :]).reshape(-1).astype(jnp.int32)
    doc_ends = jnp.cumsum(lengths).astype(jnp.int32)
    documents = jnp.sum((positions[:, None] >= doc_ends[None, :]).astype(jnp.int32), axis=1).astype(jnp.int32)
    key_block = TOK_DEV
    row_total = TOK_DEV * HQ

    def tile_step(grad_total, tile_index):
        begin_tile = (tile_index * TOK_DEV).astype(jnp.int32)
        query_rows = lax.dynamic_slice_in_dim(queries, begin_tile, TOK_DEV, 0).reshape(row_total, DH)
        cotangent_rows = lax.dynamic_slice_in_dim(grad_out, begin_tile, TOK_DEV, 0).reshape(row_total, DH)
        query_pos = jnp.repeat(lax.dynamic_slice_in_dim(positions, begin_tile, TOK_DEV, 0), HQ, total_repeat_length=row_total)
        query_doc = jnp.repeat(lax.dynamic_slice_in_dim(documents, begin_tile, TOK_DEV, 0), HQ, total_repeat_length=row_total)
        log_total = softmax_totals(query_rows, query_pos, query_doc, keys, positions, documents, key_block, score_scale)
        attended = attend_rows(query_rows, query_pos, query_doc, keys, values, positions, documents, key_block, log_total, score_scale).astype(jnp.bfloat16)
        row_delta = jnp.sum(cotangent_rows.astype(jnp.float32) * attended.astype(jnp.float32), axis=1)

        def loop_step(loop_index, carried):
            query_grad, grads = carried
            begin_row = (loop_index * key_block).astype(jnp.int32)
            key_rows = lax.dynamic_slice_in_dim(keys, begin_row, key_block, 0)
            value_rows = lax.dynamic_slice_in_dim(values, begin_row, key_block, 0)
            block_pos = lax.dynamic_slice_in_dim(positions, begin_row, key_block, 0)
            block_doc = lax.dynamic_slice_in_dim(documents, begin_row, key_block, 0)

            def update(state):
                query_grad, grads = state
                probs = block_probs(query_rows, query_pos, query_doc, key_rows, block_pos, block_doc, log_total, score_scale)
                probs_low = probs.astype(jnp.bfloat16)
                dprob = jnp.dot(cotangent_rows, value_rows.T, preferred_element_type=jnp.float32)
                dscore = (probs * (dprob - row_delta[:, None]) * score_scale).astype(jnp.bfloat16)
                query_grad = query_grad + jnp.dot(dscore, key_rows, preferred_element_type=jnp.float32)
                key_part = jnp.dot(dscore.T, query_rows, preferred_element_type=jnp.float32)
                value_part = jnp.dot(probs_low.T, cotangent_rows, preferred_element_type=jnp.float32)
                old_rows = lax.dynamic_slice_in_dim(grads, begin_row, key_block, 0)
                new_rows = old_rows + jnp.concatenate([key_part, value_part], axis=1)
                grads = lax.dynamic_update_slice(grads, new_rows, (begin_row, jnp.array(0, jnp.int32)))
                return query_grad, grads

            alive = jnp.any(live_test(query_pos, query_doc, block_pos, block_doc))
            return lax.cond(alive, update, lambda unchanged: unchanged, carried)

        start_state = (jnp.zeros((row_total, DH), jnp.float32), grad_total)
        query_grad, grad_total = lax.fori_loop(0, N_CTX, loop_step, start_state)
        return grad_total, (attended, query_grad.astype(jnp.bfloat16))

    grad_start = jnp.zeros((TOKENS, 2 * DH), jnp.float32)
    grad_total, (attended_tiles, query_tiles) = lax.scan(tile_step, grad_start, jnp.arange(N_CTX, dtype=jnp.int32))
    attended = attended_tiles.reshape(TOKENS, HQ, DH)
    grad_queries = query_tiles.reshape(TOKENS, HQ, DH)
    return attended, grad_queries, grad_total[:, :DH], grad_total[:, DH:]
```

```python
import functools
import math

import jax
import jax.numpy as jnp
from jax import lax
from jax.experimental import pallas as pl
from jax.experimental.pallas import tpu as pltpu
from jax.sharding import PartitionSpec as P

NEG_FILL = -1e30
MESH = pl.DeviceIdType.MESH
BACK = 4
KEY_BLOCK = 256
ROW_CHUNK = 256


def dot(left, right, dims):
    return lax.dot_general(left, right, (dims, ((), ())), preferred_element_type=jnp.float32)


def ctx_of(quad, z, nz):
    return (lax.div(quad, 2) * nz + z) * 2 + lax.rem(quad, 2)


def place(nz, heads):
    ctx = lax.axis_index("ctx")
    head = lax.axis_index("head")
    core = lax.rem(ctx, 2)
    z = lax.rem(lax.div(ctx, 2), nz)
    x_lo = lax.div(ctx, 2 * nz)
    quad = x_lo * 2 + core
    return quad, z, head, quad * heads + head


def greet(quad, z, head, slot, nz, heads):
    barrier = pltpu.get_barrier_semaphore()
    slots = 4 * heads

    @pl.loop(1, slots)
    def _(step):
        other = lax.rem(slot + step, slots)
        target = (ctx_of(lax.div(other, heads), z, nz), lax.rem(other, heads))
        pl.semaphore_signal(barrier, inc=1, device_id=target, device_id_type=MESH)

    @pl.loop(1, nz)
    def _(step):
        target = (ctx_of(quad, lax.rem(z + step, nz), nz), head)
        pl.semaphore_signal(barrier, inc=1, device_id=target, device_id_type=MESH)

    pl.semaphore_wait(barrier, slots - 1 + nz - 1)


def gather_kernel(
    nz,
    heads,
    tiles_ref,
    key_ref,
    value_ref,
    win_ref,
    own,
    zbuf,
    sbuf,
    load_sem,
    qs,
    qr,
    zs,
    zr,
    ps,
    pr,
):
    quad, z, head, slot = place(nz, heads)
    slots = 4 * heads
    part = own.shape[1]
    width = key_ref.shape[-1]
    loads = (
        pltpu.make_async_copy(key_ref, own.at[:, :, 0:width], load_sem.at[0]),
        pltpu.make_async_copy(value_ref, own.at[:, :, width : 2 * width], load_sem.at[1]),
    )
    for copy in loads:
        copy.start()
    greet(quad, z, head, slot, nz, heads)
    for copy in loads:
        copy.wait()

    def quad_copy(step):
        other = lax.rem(quad + step, 4)
        return pltpu.make_async_remote_copy(
            src_ref=own.at[other * heads + head],
            dst_ref=zbuf.at[z, quad],
            send_sem=qs.at[step],
            recv_sem=qr.at[step],
            device_id=(ctx_of(other, z, nz), head),
            device_id_type=MESH,
        )

    for step in range(1, 4):
        quad_copy(step).start()
    mine = pltpu.make_async_copy(own.at[slot], zbuf.at[z, quad], load_sem.at[0])
    whole = pltpu.make_async_copy(own, win_ref.at[BACK], load_sem.at[1])
    mine.start()
    whole.start()
    mine.wait()
    for step in range(1, 4):
        quad_copy(step).wait()

    def z_copy(step):
        return pltpu.make_async_remote_copy(
            src_ref=zbuf.at[z],
            dst_ref=zbuf.at[z],
            send_sem=zs.at[step],
            recv_sem=zr.at[step],
            device_id=(ctx_of(quad, lax.rem(z + step, nz), nz), head),
            device_id_type=MESH,
        )

    @pl.loop(1, nz)
    def _(step):
        z_copy(step).start()

    count = 4 * nz
    wanted = []
    for other in range(4):
        tile = tiles_ref[ctx_of(other, z, nz)]
        for back in range(BACK):
            wanted.append(jnp.maximum(tile - BACK + back, 0))

    def find(index, found):
        tile = tiles_ref[index]
        return tuple(jnp.where(tile == want, index, have) for want, have in zip(wanted, found))

    holders = lax.fori_loop(0, count, find, tuple(jnp.int32(0) for _ in wanted))

    @pl.loop(1, nz)
    def _(step):
        z_copy(step).wait()

    for other in range(4):
        for back in range(BACK):
            holder = holders[other * BACK + back]
            from_z = lax.rem(lax.div(holder, 2), nz)
            from_quad = lax.div(holder, 2 * nz) * 2 + lax.rem(holder, 2)
            sbuf[other, back] = zbuf[from_z, from_quad]

    def plane_copy(step):
        other = lax.rem(slot + step, slots)
        return pltpu.make_async_remote_copy(
            src_ref=sbuf.at[lax.div(other, heads)],
            dst_ref=win_ref.at[0:BACK, slot],
            send_sem=ps.at[step],
            recv_sem=pr.at[step],
            device_id=(ctx_of(lax.div(other, heads), z, nz), lax.rem(other, heads)),
            device_id_type=MESH,
        )

    @pl.loop(1, slots)
    def _(step):
        plane_copy(step).start()

    mine = pltpu.make_async_copy(sbuf.at[quad], win_ref.at[0:BACK, slot], load_sem.at[0])
    mine.start()
    whole.wait()
    mine.wait()

    @pl.loop(1, slots)
    def _(step):
        plane_copy(step).wait()


def gather_window(keys, values, tile_of, nz, heads):
    rows, width = keys.shape
    slots = 4 * heads
    part = rows // slots
    block = (part, 2 * width)
    return pl.pallas_call(
        functools.partial(gather_kernel, nz, heads),
        out_shape=jax.ShapeDtypeStruct((BACK + 1, slots) + block, keys.dtype),
        in_specs=[
            pl.BlockSpec(memory_space=pltpu.SMEM),
            pl.BlockSpec(memory_space=pl.ANY),
            pl.BlockSpec(memory_space=pl.ANY),
        ],
        out_specs=pl.BlockSpec(memory_space=pltpu.VMEM),
        scratch_shapes=[
            pltpu.VMEM((slots,) + block, keys.dtype),
            pltpu.VMEM((nz, 4) + block, keys.dtype),
            pltpu.VMEM((4, BACK) + block, keys.dtype),
            pltpu.SemaphoreType.DMA((2,)),
            pltpu.SemaphoreType.DMA((4,)),
            pltpu.SemaphoreType.DMA((4,)),
            pltpu.SemaphoreType.DMA((nz,)),
            pltpu.SemaphoreType.DMA((nz,)),
            pltpu.SemaphoreType.DMA((slots,)),
            pltpu.SemaphoreType.DMA((slots,)),
        ],
        compiler_params=pltpu.CompilerParams(collective_id=0, has_side_effects=True),
        name="gather_window",
    )(tile_of, keys.reshape(slots, part, width), values.reshape(slots, part, width))


def reduce_kernel(
    nz, heads, tiles_ref, grad_ref, out_ref, rbuf, acc, zsend, zrecv, res, load_sem, gs, gr, zs, zr, fs, fr
):
    quad, z, head, slot = place(nz, heads)
    slots = 4 * heads
    greet(quad, z, head, slot, nz, heads)

    def term_copy(step):
        other = lax.rem(slot + step, slots)
        return pltpu.make_async_remote_copy(
            src_ref=grad_ref.at[:, other],
            dst_ref=rbuf.at[slot],
            send_sem=gs.at[step],
            recv_sem=gr.at[step],
            device_id=(ctx_of(lax.div(other, heads), z, nz), lax.rem(other, heads)),
            device_id_type=MESH,
        )

    @pl.loop(1, slots)
    def _(step):
        term_copy(step).start()

    mine = pltpu.make_async_copy(grad_ref.at[:, slot], rbuf.at[slot], load_sem)
    mine.start()
    mine.wait()

    @pl.loop(1, slots)
    def _(step):
        term_copy(step).wait()

    for other in range(4):
        for back in range(BACK + 1):
            total = rbuf[other * heads, back].astype(jnp.float32)
            for index in range(1, heads):
                total = total + rbuf[other * heads + index, back].astype(jnp.float32)
            acc[other, back] = total

    sources = [tiles_ref[ctx_of(other, z, nz)] - BACK for other in range(4)]

    @pl.loop(0, nz)
    def _(to_z):
        for to_quad in range(4):
            tile = tiles_ref[ctx_of(to_quad, to_z, nz)]
            total = None
            for other in range(4):
                back = tile - sources[other]
                inside = jnp.logical_and(back >= 0, back <= BACK)
                loaded = acc[other, jnp.clip(back, 0, BACK)]
                term = jnp.where(inside, loaded, 0.0)
                total = term if total is None else total + term
            zsend[to_z, to_quad] = total.astype(zsend.dtype)

    def z_copy(step):
        to_z = lax.rem(z + step, nz)
        return pltpu.make_async_remote_copy(
            src_ref=zsend.at[to_z],
            dst_ref=zrecv.at[z],
            send_sem=zs.at[step],
            recv_sem=zr.at[step],
            device_id=(ctx_of(quad, to_z, nz), head),
            device_id_type=MESH,
        )

    @pl.loop(1, nz)
    def _(step):
        z_copy(step).start()

    mine = pltpu.make_async_copy(zsend.at[z], zrecv.at[z], load_sem)
    mine.start()
    mine.wait()

    @pl.loop(1, nz)
    def _(step):
        z_copy(step).wait()

    total = zrecv[0].astype(jnp.float32)
    for index in range(1, nz):
        total = total + zrecv[index].astype(jnp.float32)
    res[...] = total.astype(res.dtype)

    def final_copy(step):
        other = lax.rem(slot + step, slots)
        return pltpu.make_async_remote_copy(
            src_ref=res.at[lax.div(other, heads)],
            dst_ref=out_ref.at[slot],
            send_sem=fs.at[step],
            recv_sem=fr.at[step],
            device_id=(ctx_of(lax.div(other, heads), z, nz), lax.rem(other, heads)),
            device_id_type=MESH,
        )

    @pl.loop(1, slots)
    def _(step):
        final_copy(step).start()

    mine = pltpu.make_async_copy(res.at[quad], out_ref.at[slot], load_sem)
    mine.start()
    mine.wait()

    @pl.loop(1, slots)
    def _(step):
        final_copy(step).wait()


def reduce_terms(terms, tile_of, nz, heads):
    slots = 4 * heads
    block = terms.shape[2:]
    low = terms.dtype
    return pl.pallas_call(
        functools.partial(reduce_kernel, nz, heads),
        out_shape=jax.ShapeDtypeStruct((slots,) + block, low),
        in_specs=[
            pl.BlockSpec(memory_space=pltpu.SMEM),
            pl.BlockSpec(memory_space=pltpu.VMEM),
        ],
        out_specs=pl.BlockSpec(memory_space=pltpu.VMEM),
        scratch_shapes=[
            pltpu.VMEM((slots, BACK + 1) + block, low),
            pltpu.VMEM((4, BACK + 1) + block, jnp.float32),
            pltpu.VMEM((nz, 4) + block, low),
            pltpu.VMEM((nz, 4) + block, low),
            pltpu.VMEM((4,) + block, low),
            pltpu.SemaphoreType.DMA,
            pltpu.SemaphoreType.DMA((slots,)),
            pltpu.SemaphoreType.DMA((slots,)),
            pltpu.SemaphoreType.DMA((nz,)),
            pltpu.SemaphoreType.DMA((nz,)),
            pltpu.SemaphoreType.DMA((slots,)),
            pltpu.SemaphoreType.DMA((slots,)),
        ],
        compiler_params=pltpu.CompilerParams(collective_id=1, has_side_effects=True),
        name="reduce_terms",
    )(tile_of, terms)


def attention_kernel(
    local_heads,
    own_ctx_ref,
    tiles_ref,
    lengths_ref,
    query_ref,
    cot_ref,
    win_ref,
    att_ref,
    dq_ref,
    grad_ref,
    s_scr,
    p_scr,
    dk_acc,
    dv_acc,
):
    row_total, width = query_ref.shape
    keys_total = win_ref.shape[0]
    tile_rows = row_total // local_heads
    scale = float(width) ** -0.5
    log_scale = scale * math.log2(math.e)
    tile = tiles_ref[own_ctx_ref[0]]
    base = (tile - BACK) * tile_rows
    chunk_pos = ROW_CHUNK // local_heads
    dk_acc[...] = jnp.zeros_like(dk_acc)
    dv_acc[...] = jnp.zeros_like(dv_acc)
    doc_ends = []
    running = jnp.int32(0)
    for index in range(lengths_ref.shape[0]):
        running = running + lengths_ref[index]
        doc_ends.append(running)

    for chunk in range(row_total // ROW_CHUNK):
        rows = pl.ds(chunk * ROW_CHUNK, ROW_CHUNK)
        first_pos = tile * tile_rows + chunk * chunk_pos
        pos = first_pos + lax.broadcasted_iota(jnp.int32, (1, ROW_CHUNK), 1) // local_heads
        low = jnp.zeros_like(pos)
        low_first = jnp.int32(0)
        for end in doc_ends:
            low = jnp.where(pos >= end, end, low)
            low_first = jnp.where(first_pos >= end, end, low_first)
        low = low - base
        high = pos - base
        first_block = (low_first - base) // KEY_BLOCK
        last_block = (BACK * tile_rows + (chunk + 1) * chunk_pos + KEY_BLOCK - 1) // KEY_BLOCK
        q = query_ref[rows, :]

        def score_step(block, top):
            begin = pl.multiple_of(block * KEY_BLOCK, KEY_BLOCK)
            k = win_ref[pl.ds(begin, KEY_BLOCK), 0:width]
            s = dot(k, q, ((1,), (1,)))
            at = begin + lax.broadcasted_iota(jnp.int32, s.shape, 0)
            s = jnp.where((at >= low) & (at <= high), s, NEG_FILL)
            s_scr[pl.ds(begin, KEY_BLOCK), :] = s
            return jnp.maximum(top, jnp.max(s.reshape(KEY_BLOCK // 8, 8, ROW_CHUNK), axis=0))

        top = lax.fori_loop(
            first_block, last_block, score_step, jnp.full((8, ROW_CHUNK), NEG_FILL, jnp.float32)
        )
        top = jnp.max(top, axis=0, keepdims=True) * log_scale

        def prob_step(block, carried):
            total, out = carried
            begin = pl.multiple_of(block * KEY_BLOCK, KEY_BLOCK)
            p = jnp.exp2(s_scr[pl.ds(begin, KEY_BLOCK), :] * log_scale - top)
            total = total + jnp.sum(p.reshape(KEY_BLOCK // 8, 8, ROW_CHUNK), axis=0)
            p_low = p.astype(jnp.bfloat16)
            p_scr[pl.ds(begin, KEY_BLOCK), :] = p_low
            v = win_ref[pl.ds(begin, KEY_BLOCK), width : 2 * width]
            return total, out + dot(v, p_low, ((0,), (0,)))

        total, out = lax.fori_loop(
            first_block,
            last_block,
            prob_step,
            (jnp.zeros((8, ROW_CHUNK), jnp.float32), jnp.zeros((width, ROW_CHUNK), jnp.float32)),
        )
        inverse = 1.0 / jnp.sum(total, axis=0, keepdims=True)
        out = (out * inverse).astype(jnp.bfloat16).astype(jnp.float32)
        att_ref[rows, :] = out.T.astype(jnp.bfloat16)
        cot = cot_ref[rows, :].astype(jnp.float32).T
        delta = jnp.sum(cot * out, axis=0, keepdims=True) * inverse
        cot_scaled = cot * inverse
        cot_low = cot_scaled.astype(jnp.bfloat16)
        cot_rows = cot_scaled.T.astype(jnp.bfloat16)

        def grad_step(block, dq):
            begin = pl.multiple_of(block * KEY_BLOCK, KEY_BLOCK)
            keys_at = pl.ds(begin, KEY_BLOCK)
            k = win_ref[keys_at, 0:width]
            v = win_ref[keys_at, width : 2 * width]
            p_low = p_scr[keys_at, :]
            dp = dot(v, cot_low, ((1,), (0,)))
            ds = (p_low.astype(jnp.float32) * (dp - delta)).astype(jnp.bfloat16)
            dv_acc[keys_at, :] += dot(p_low, cot_rows, ((1,), (0,)))
            dk_acc[keys_at, :] += dot(ds, q, ((1,), (0,)))
            return dq + dot(k, ds, ((0,), (0,)))

        dq = lax.fori_loop(
            first_block, last_block, grad_step, jnp.zeros((width, ROW_CHUNK), jnp.float32)
        )
        dq_ref[rows, :] = (dq * scale).T.astype(jnp.bfloat16)

    grad_ref[:, 0:width] = (dk_acc[...] * scale).astype(jnp.bfloat16)
    grad_ref[:, width : 2 * width] = dv_acc[...].astype(jnp.bfloat16)


def attention(own_ctx, tile_of, lengths, query_rows, cot_rows, window, local_heads):
    row_total, width = query_rows.shape
    keys_total = window.shape[0]
    smem = pl.BlockSpec(memory_space=pltpu.SMEM)
    vmem = pl.BlockSpec(memory_space=pltpu.VMEM)
    return pl.pallas_call(
        functools.partial(attention_kernel, local_heads),
        out_shape=(
            jax.ShapeDtypeStruct((row_total, width), jnp.bfloat16),
            jax.ShapeDtypeStruct((row_total, width), jnp.bfloat16),
            jax.ShapeDtypeStruct((keys_total, 2 * width), jnp.bfloat16),
        ),
        in_specs=[smem, smem, smem, vmem, vmem, vmem],
        out_specs=(vmem, vmem, vmem),
        scratch_shapes=[
            pltpu.VMEM((keys_total, ROW_CHUNK), jnp.float32),
            pltpu.VMEM((keys_total, ROW_CHUNK), jnp.bfloat16),
            pltpu.VMEM((keys_total, width), jnp.float32),
            pltpu.VMEM((keys_total, width), jnp.float32),
        ],
        compiler_params=pltpu.CompilerParams(vmem_limit_bytes=40 * 1024 * 1024),
        name="attention",
    )(own_ctx, tile_of, lengths, query_rows, cot_rows, window)


def on_device(ctx_count, heads, queries, keys, values, grad_out, lengths, tile_of):
    tile_rows, local_heads, width = queries.shape
    nz = ctx_count // 4
    slots = 4 * heads
    part = tile_rows // slots
    window = gather_window(keys, values, tile_of, nz, heads)
    own_ctx = lax.axis_index("ctx").astype(jnp.int32).reshape(1)
    attended, query_grad, terms = attention(
        own_ctx,
        tile_of,
        lengths,
        queries.reshape(-1, width),
        grad_out.reshape(-1, width),
        window.reshape((BACK + 1) * tile_rows, 2 * width),
        local_heads,
    )
    sums = reduce_terms(
        terms.reshape(BACK + 1, slots, part, 2 * width), tile_of, nz, heads
    ).reshape(tile_rows, 2 * width)
    return (
        attended.reshape(queries.shape),
        query_grad.reshape(queries.shape),
        sums[:, :width].astype(jnp.float32),
        sums[:, width:].astype(jnp.float32),
    )


def solution(mesh):
    return jax.shard_map(
        functools.partial(on_device, mesh.shape["ctx"], mesh.shape["head"]),
        mesh=mesh,
        in_specs=(
            P("ctx", "head", None),
            P("ctx", None),
            P("ctx", None),
            P("ctx", "head", None),
            P(),
            P(),
        ),
        out_specs=(P("ctx", "head", None), P("ctx", "head", None), P("ctx", None), P("ctx", None)),
        check_vma=False,
    )
```

```python
import functools
import math

import jax
import jax.numpy as jnp
from jax import lax
from jax.experimental import pallas as pl
from jax.experimental.pallas import tpu as pltpu
from jax.sharding import PartitionSpec as P

NEG_FILL = -1e30
MESH = pl.DeviceIdType.MESH
BACK = 4
KEY_BLOCK = 512
ROW_CHUNK = 1024


def dot(left, right, dims):
    return lax.dot_general(left, right, (dims, ((), ())), preferred_element_type=jnp.float32)


def ctx_of(quad, z, nz):
    return (lax.div(quad, 2) * nz + z) * 2 + lax.rem(quad, 2)


def place(nz, heads):
    ctx = lax.axis_index("ctx")
    head = lax.axis_index("head")
    core = lax.rem(ctx, 2)
    z = lax.rem(lax.div(ctx, 2), nz)
    x_lo = lax.div(ctx, 2 * nz)
    quad = x_lo * 2 + core
    return quad, z, head, quad * heads + head


def greet(quad, z, head, slot, nz, heads):
    barrier = pltpu.get_barrier_semaphore()
    slots = 4 * heads

    @pl.loop(1, slots)
    def _(step):
        other = lax.rem(slot + step, slots)
        target = (ctx_of(lax.div(other, heads), z, nz), lax.rem(other, heads))
        pl.semaphore_signal(barrier, inc=1, device_id=target, device_id_type=MESH)

    @pl.loop(1, nz)
    def _(step):
        target = (ctx_of(quad, lax.rem(z + step, nz), nz), head)
        pl.semaphore_signal(barrier, inc=1, device_id=target, device_id_type=MESH)

    pl.semaphore_wait(barrier, slots - 1 + nz - 1)


def gather_kernel(
    nz,
    heads,
    tiles_ref,
    key_ref,
    value_ref,
    win_ref,
    own,
    zbuf,
    sbuf,
    load_sem,
    qs,
    qr,
    zs,
    zr,
    ps,
    pr,
):
    quad, z, head, slot = place(nz, heads)
    slots = 4 * heads
    part = own.shape[1]
    width = key_ref.shape[-1]
    loads = (
        pltpu.make_async_copy(key_ref, own.at[:, :, 0:width], load_sem.at[0]),
        pltpu.make_async_copy(value_ref, own.at[:, :, width : 2 * width], load_sem.at[1]),
    )
    for copy in loads:
        copy.start()
    greet(quad, z, head, slot, nz, heads)
    for copy in loads:
        copy.wait()

    def quad_copy(step):
        other = lax.rem(quad + step, 4)
        return pltpu.make_async_remote_copy(
            src_ref=own.at[other * heads + head],
            dst_ref=zbuf.at[z, quad],
            send_sem=qs.at[step],
            recv_sem=qr.at[step],
            device_id=(ctx_of(other, z, nz), head),
            device_id_type=MESH,
        )

    for step in range(1, 4):
        quad_copy(step).start()
    mine = pltpu.make_async_copy(own.at[slot], zbuf.at[z, quad], load_sem.at[0])
    whole = pltpu.make_async_copy(own, win_ref.at[BACK], load_sem.at[1])
    mine.start()
    whole.start()
    mine.wait()
    for step in range(1, 4):
        quad_copy(step).wait()

    def z_copy(step):
        return pltpu.make_async_remote_copy(
            src_ref=zbuf.at[z],
            dst_ref=zbuf.at[z],
            send_sem=zs.at[step],
            recv_sem=zr.at[step],
            device_id=(ctx_of(quad, lax.rem(z + step, nz), nz), head),
            device_id_type=MESH,
        )

    @pl.loop(1, nz)
    def _(step):
        z_copy(step).start()

    count = 4 * nz
    wanted = []
    for other in range(4):
        tile = tiles_ref[ctx_of(other, z, nz)]
        for back in range(BACK):
            wanted.append(jnp.maximum(tile - BACK + back, 0))

    def find(index, found):
        tile = tiles_ref[index]
        return tuple(jnp.where(tile == want, index, have) for want, have in zip(wanted, found))

    holders = lax.fori_loop(0, count, find, tuple(jnp.int32(0) for _ in wanted))

    @pl.loop(1, nz)
    def _(step):
        z_copy(step).wait()

    for other in range(4):
        for back in range(BACK):
            holder = holders[other * BACK + back]
            from_z = lax.rem(lax.div(holder, 2), nz)
            from_quad = lax.div(holder, 2 * nz) * 2 + lax.rem(holder, 2)
            sbuf[other, back] = zbuf[from_z, from_quad]

    def plane_copy(step):
        other = lax.rem(slot + step, slots)
        return pltpu.make_async_remote_copy(
            src_ref=sbuf.at[lax.div(other, heads)],
            dst_ref=win_ref.at[0:BACK, slot],
            send_sem=ps.at[step],
            recv_sem=pr.at[step],
            device_id=(ctx_of(lax.div(other, heads), z, nz), lax.rem(other, heads)),
            device_id_type=MESH,
        )

    @pl.loop(1, slots)
    def _(step):
        plane_copy(step).start()

    mine = pltpu.make_async_copy(sbuf.at[quad], win_ref.at[0:BACK, slot], load_sem.at[0])
    mine.start()
    whole.wait()
    mine.wait()

    @pl.loop(1, slots)
    def _(step):
        plane_copy(step).wait()


def gather_window(keys, values, tile_of, nz, heads):
    rows, width = keys.shape
    slots = 4 * heads
    part = rows // slots
    block = (part, 2 * width)
    return pl.pallas_call(
        functools.partial(gather_kernel, nz, heads),
        out_shape=jax.ShapeDtypeStruct((BACK + 1, slots) + block, keys.dtype),
        in_specs=[
            pl.BlockSpec(memory_space=pltpu.SMEM),
            pl.BlockSpec(memory_space=pl.ANY),
            pl.BlockSpec(memory_space=pl.ANY),
        ],
        out_specs=pl.BlockSpec(memory_space=pltpu.VMEM),
        scratch_shapes=[
            pltpu.VMEM((slots,) + block, keys.dtype),
            pltpu.VMEM((nz, 4) + block, keys.dtype),
            pltpu.VMEM((4, BACK) + block, keys.dtype),
            pltpu.SemaphoreType.DMA((2,)),
            pltpu.SemaphoreType.DMA((4,)),
            pltpu.SemaphoreType.DMA((4,)),
            pltpu.SemaphoreType.DMA((nz,)),
            pltpu.SemaphoreType.DMA((nz,)),
            pltpu.SemaphoreType.DMA((slots,)),
            pltpu.SemaphoreType.DMA((slots,)),
        ],
        compiler_params=pltpu.CompilerParams(collective_id=0, has_side_effects=True),
        name="gather_window",
    )(tile_of, keys.reshape(slots, part, width), values.reshape(slots, part, width))


def reduce_kernel(
    nz, heads, tiles_ref, grad_ref, out_ref, rbuf, acc, zsend, zrecv, res, load_sem, gs, gr, zs, zr, fs, fr
):
    quad, z, head, slot = place(nz, heads)
    slots = 4 * heads
    greet(quad, z, head, slot, nz, heads)

    def term_copy(step):
        other = lax.rem(slot + step, slots)
        return pltpu.make_async_remote_copy(
            src_ref=grad_ref.at[:, other],
            dst_ref=rbuf.at[slot],
            send_sem=gs.at[step],
            recv_sem=gr.at[step],
            device_id=(ctx_of(lax.div(other, heads), z, nz), lax.rem(other, heads)),
            device_id_type=MESH,
        )

    @pl.loop(1, slots)
    def _(step):
        term_copy(step).start()

    mine = pltpu.make_async_copy(grad_ref.at[:, slot], rbuf.at[slot], load_sem)
    mine.start()
    mine.wait()

    @pl.loop(1, slots)
    def _(step):
        term_copy(step).wait()

    for other in range(4):
        for back in range(BACK + 1):
            total = rbuf[other * heads, back].astype(jnp.float32)
            for index in range(1, heads):
                total = total + rbuf[other * heads + index, back].astype(jnp.float32)
            acc[other, back] = total

    sources = [tiles_ref[ctx_of(other, z, nz)] - BACK for other in range(4)]

    @pl.loop(0, nz)
    def _(to_z):
        for to_quad in range(4):
            tile = tiles_ref[ctx_of(to_quad, to_z, nz)]
            total = None
            for other in range(4):
                back = tile - sources[other]
                inside = jnp.logical_and(back >= 0, back <= BACK)
                loaded = acc[other, jnp.clip(back, 0, BACK)]
                term = jnp.where(inside, loaded, 0.0)
                total = term if total is None else total + term
            zsend[to_z, to_quad] = total.astype(zsend.dtype)

    def z_copy(step):
        to_z = lax.rem(z + step, nz)
        return pltpu.make_async_remote_copy(
            src_ref=zsend.at[to_z],
            dst_ref=zrecv.at[z],
            send_sem=zs.at[step],
            recv_sem=zr.at[step],
            device_id=(ctx_of(quad, to_z, nz), head),
            device_id_type=MESH,
        )

    @pl.loop(1, nz)
    def _(step):
        z_copy(step).start()

    mine = pltpu.make_async_copy(zsend.at[z], zrecv.at[z], load_sem)
    mine.start()
    mine.wait()

    @pl.loop(1, nz)
    def _(step):
        z_copy(step).wait()

    total = zrecv[0].astype(jnp.float32)
    for index in range(1, nz):
        total = total + zrecv[index].astype(jnp.float32)
    res[...] = total.astype(res.dtype)

    def final_copy(step):
        other = lax.rem(slot + step, slots)
        return pltpu.make_async_remote_copy(
            src_ref=res.at[lax.div(other, heads)],
            dst_ref=out_ref.at[slot],
            send_sem=fs.at[step],
            recv_sem=fr.at[step],
            device_id=(ctx_of(lax.div(other, heads), z, nz), lax.rem(other, heads)),
            device_id_type=MESH,
        )

    @pl.loop(1, slots)
    def _(step):
        final_copy(step).start()

    mine = pltpu.make_async_copy(res.at[quad], out_ref.at[slot], load_sem)
    mine.start()
    mine.wait()

    @pl.loop(1, slots)
    def _(step):
        final_copy(step).wait()


def reduce_terms(terms, tile_of, nz, heads):
    slots = 4 * heads
    block = terms.shape[2:]
    low = terms.dtype
    return pl.pallas_call(
        functools.partial(reduce_kernel, nz, heads),
        out_shape=jax.ShapeDtypeStruct((slots,) + block, low),
        in_specs=[
            pl.BlockSpec(memory_space=pltpu.SMEM),
            pl.BlockSpec(memory_space=pltpu.VMEM),
        ],
        out_specs=pl.BlockSpec(memory_space=pltpu.VMEM),
        scratch_shapes=[
            pltpu.VMEM((slots, BACK + 1) + block, low),
            pltpu.VMEM((4, BACK + 1) + block, jnp.float32),
            pltpu.VMEM((nz, 4) + block, low),
            pltpu.VMEM((nz, 4) + block, low),
            pltpu.VMEM((4,) + block, low),
            pltpu.SemaphoreType.DMA,
            pltpu.SemaphoreType.DMA((slots,)),
            pltpu.SemaphoreType.DMA((slots,)),
            pltpu.SemaphoreType.DMA((nz,)),
            pltpu.SemaphoreType.DMA((nz,)),
            pltpu.SemaphoreType.DMA((slots,)),
            pltpu.SemaphoreType.DMA((slots,)),
        ],
        compiler_params=pltpu.CompilerParams(collective_id=1, has_side_effects=True),
        name="reduce_terms",
    )(tile_of, terms)


def attention_kernel(
    local_heads,
    own_ctx_ref,
    tiles_ref,
    lengths_ref,
    query_ref,
    cot_ref,
    win_ref,
    att_ref,
    dq_ref,
    grad_ref,
    s_scr,
    p_scr,
    dk_acc,
    dv_acc,
):
    row_total, width = query_ref.shape
    keys_total = win_ref.shape[0]
    tile_rows = row_total // local_heads
    scale = float(width) ** -0.5
    log_scale = scale * math.log2(math.e)
    tile = tiles_ref[own_ctx_ref[0]]
    base = (tile - BACK) * tile_rows
    chunk_pos = ROW_CHUNK // local_heads
    doc_ends = []
    running = jnp.int32(0)
    for index in range(lengths_ref.shape[0]):
        running = running + lengths_ref[index]
        doc_ends.append(running)

    for chunk in range(row_total // ROW_CHUNK):
        rows = pl.ds(chunk * ROW_CHUNK, ROW_CHUNK)
        first_pos = tile * tile_rows + chunk * chunk_pos
        pos = first_pos + lax.broadcasted_iota(jnp.int32, (1, ROW_CHUNK), 1) // local_heads
        low = jnp.zeros_like(pos)
        for end in doc_ends:
            low = jnp.where(pos >= end, end, low)
        low = low - base
        high = pos - base
        q = query_ref[rows, :]
        blocks = range(0, keys_total, KEY_BLOCK)
        top = jnp.full((8, ROW_CHUNK), NEG_FILL, jnp.float32)
        at = lax.broadcasted_iota(jnp.int32, (KEY_BLOCK, ROW_CHUNK), 0)
        for begin in blocks:
            keys_at = pl.ds(begin, KEY_BLOCK)
            s = dot(win_ref[keys_at, 0:width], q, ((1,), (1,)))
            live = at >= low - begin
            if begin + KEY_BLOCK > BACK * tile_rows:
                live = live & (at <= high - begin)
            s = jnp.where(live, s, NEG_FILL)
            s_scr[keys_at, :] = s
            top = jnp.maximum(top, jnp.max(s.reshape(KEY_BLOCK // 8, 8, ROW_CHUNK), axis=0))
        top = jnp.max(top, axis=0, keepdims=True) * log_scale
        total = jnp.zeros((8, ROW_CHUNK), jnp.float32)
        out = jnp.zeros((width, ROW_CHUNK), jnp.float32)
        for begin in blocks:
            keys_at = pl.ds(begin, KEY_BLOCK)
            p = jnp.exp2(s_scr[keys_at, :] * log_scale - top)
            total = total + jnp.sum(p.reshape(KEY_BLOCK // 8, 8, ROW_CHUNK), axis=0)
            p_low = p.astype(jnp.bfloat16)
            p_scr[keys_at, :] = p_low
            out = out + dot(win_ref[keys_at, width : 2 * width], p_low, ((0,), (0,)))
        inverse = 1.0 / jnp.sum(total, axis=0, keepdims=True)
        out = (out * inverse).astype(jnp.bfloat16).astype(jnp.float32)
        att_ref[rows, :] = out.T.astype(jnp.bfloat16)
        cot = cot_ref[rows, :].astype(jnp.float32).T
        delta = jnp.sum(cot * out, axis=0, keepdims=True) * inverse
        cot_scaled = cot * inverse
        cot_low = cot_scaled.astype(jnp.bfloat16)
        cot_rows = cot_scaled.T.astype(jnp.bfloat16)
        dq = jnp.zeros((width, ROW_CHUNK), jnp.float32)
        for begin in blocks:
            keys_at = pl.ds(begin, KEY_BLOCK)
            k = win_ref[keys_at, 0:width]
            v = win_ref[keys_at, width : 2 * width]
            p_low = p_scr[keys_at, :]
            dp = dot(v, cot_low, ((1,), (0,)))
            ds = (p_low.astype(jnp.float32) * (dp - delta)).astype(jnp.bfloat16)
            grad_ref[keys_at, width : 2 * width] = dot(p_low, cot_rows, ((1,), (0,))).astype(jnp.bfloat16)
            grad_ref[keys_at, 0:width] = (dot(ds, q, ((1,), (0,))) * scale).astype(jnp.bfloat16)
            dq = dq + dot(k, ds, ((0,), (0,)))
        dq_ref[rows, :] = (dq * scale).T.astype(jnp.bfloat16)


def attention(own_ctx, tile_of, lengths, query_rows, cot_rows, window, local_heads):
    row_total, width = query_rows.shape
    keys_total = window.shape[0]
    smem = pl.BlockSpec(memory_space=pltpu.SMEM)
    vmem = pl.BlockSpec(memory_space=pltpu.VMEM)
    return pl.pallas_call(
        functools.partial(attention_kernel, local_heads),
        out_shape=(
            jax.ShapeDtypeStruct((row_total, width), jnp.bfloat16),
            jax.ShapeDtypeStruct((row_total, width), jnp.bfloat16),
            jax.ShapeDtypeStruct((keys_total, 2 * width), jnp.bfloat16),
        ),
        in_specs=[smem, smem, smem, vmem, vmem, vmem],
        out_specs=(vmem, vmem, vmem),
        scratch_shapes=[
            pltpu.VMEM((keys_total, ROW_CHUNK), jnp.float32),
            pltpu.VMEM((keys_total, ROW_CHUNK), jnp.bfloat16),
            pltpu.VMEM((keys_total, width), jnp.float32),
            pltpu.VMEM((keys_total, width), jnp.float32),
        ],
        compiler_params=pltpu.CompilerParams(vmem_limit_bytes=40 * 1024 * 1024),
        name="attention",
    )(own_ctx, tile_of, lengths, query_rows, cot_rows, window)


def on_device(ctx_count, heads, queries, keys, values, grad_out, lengths, tile_of):
    tile_rows, local_heads, width = queries.shape
    nz = ctx_count // 4
    slots = 4 * heads
    part = tile_rows // slots
    window = gather_window(keys, values, tile_of, nz, heads)
    own_ctx = lax.axis_index("ctx").astype(jnp.int32).reshape(1)
    attended, query_grad, terms = attention(
        own_ctx,
        tile_of,
        lengths,
        queries.reshape(-1, width),
        grad_out.reshape(-1, width),
        window.reshape((BACK + 1) * tile_rows, 2 * width),
        local_heads,
    )
    sums = reduce_terms(
        terms.reshape(BACK + 1, slots, part, 2 * width), tile_of, nz, heads
    ).reshape(tile_rows, 2 * width)
    return (
        attended.reshape(queries.shape),
        query_grad.reshape(queries.shape),
        sums[:, :width].astype(jnp.float32),
        sums[:, width:].astype(jnp.float32),
    )


def solution(mesh):
    return jax.shard_map(
        functools.partial(on_device, mesh.shape["ctx"], mesh.shape["head"]),
        mesh=mesh,
        in_specs=(
            P("ctx", "head", None),
            P("ctx", None),
            P("ctx", None),
            P("ctx", "head", None),
            P(),
            P(),
        ),
        out_specs=(P("ctx", "head", None), P("ctx", "head", None), P("ctx", None), P("ctx", None)),
        check_vma=False,
    )
```

```python
import functools
import math

import jax
import jax.numpy as jnp
from jax import lax
from jax.experimental import pallas as pl
from jax.experimental.pallas import tpu as pltpu
from jax.sharding import PartitionSpec as P

NEG_FILL = -1e30
MESH = pl.DeviceIdType.MESH
BACK = 4


def dot(left, right, dims):
    return lax.dot_general(left, right, (dims, ((), ())), preferred_element_type=jnp.float32)


def ctx_of(quad, z, nz):
    return (lax.div(quad, 2) * nz + z) * 2 + lax.rem(quad, 2)


def place(nz, heads):
    ctx = lax.axis_index("ctx")
    head = lax.axis_index("head")
    core = lax.rem(ctx, 2)
    z = lax.rem(lax.div(ctx, 2), nz)
    x_lo = lax.div(ctx, 2 * nz)
    quad = x_lo * 2 + core
    return quad, z, head, quad * heads + head


def greet(quad, z, head, slot, nz, heads):
    barrier = pltpu.get_barrier_semaphore()
    slots = 4 * heads

    @pl.loop(1, slots)
    def _(step):
        other = lax.rem(slot + step, slots)
        target = (ctx_of(lax.div(other, heads), z, nz), lax.rem(other, heads))
        pl.semaphore_signal(barrier, inc=1, device_id=target, device_id_type=MESH)

    @pl.loop(1, nz)
    def _(step):
        target = (ctx_of(quad, lax.rem(z + step, nz), nz), head)
        pl.semaphore_signal(barrier, inc=1, device_id=target, device_id_type=MESH)

    pl.semaphore_wait(barrier, slots - 1 + nz - 1)


def fused_kernel(
    nz,
    heads,
    local_heads,
    tiles_ref,
    lengths_ref,
    key_ref,
    value_ref,
    query_ref,
    cot_ref,
    att_ref,
    dq_ref,
    out_ref,
    win,
    q_scr,
    c_scr,
    zbuf,
    sbuf,
    s_scr,
    p_scr,
    dp_own,
    cot_t,
    low_scr,
    att_scr,
    dq_scr,
    terms,
    rbuf,
    acc,
    zsend,
    zrecv,
    res,
    load_sem,
    send_sem,
    recv_sem,
):
    quad, z, head, slot = place(nz, heads)
    slots, part, width2 = win.shape[1:]
    width = width2 // 2
    rows = query_ref.shape[0]
    tile_rows = slots * part
    scale = float(width) ** -0.5
    log_scale = scale * math.log2(math.e)

    def plane_target(step):
        other = lax.rem(slot + step, slots)
        other_quad = lax.div(other, heads)
        return other, other_quad, (ctx_of(other_quad, z, nz), lax.rem(other, heads))

    def arrived(phase, like):
        pltpu.make_async_copy(like, like, recv_sem.at[phase]).wait()
        pltpu.make_async_copy(like, like, send_sem.at[phase]).wait()

    loads = (
        pltpu.make_async_copy(key_ref, win.at[BACK, :, :, 0:width], load_sem.at[0]),
        pltpu.make_async_copy(value_ref, win.at[BACK, :, :, width:width2], load_sem.at[1]),
        pltpu.make_async_copy(query_ref, q_scr, load_sem.at[2]),
        pltpu.make_async_copy(cot_ref, c_scr, load_sem.at[3]),
    )
    for copy in loads:
        copy.start()
    greet(quad, z, head, slot, nz, heads)
    loads[0].wait()
    loads[1].wait()

    for step in range(1, 4):
        other = lax.rem(quad + step, 4)
        pltpu.make_async_remote_copy(
            src_ref=win.at[BACK, other * heads + head],
            dst_ref=zbuf.at[z, quad],
            send_sem=send_sem.at[0],
            recv_sem=recv_sem.at[0],
            device_id=(ctx_of(other, z, nz), head),
            device_id_type=MESH,
        ).start()
    mine = pltpu.make_async_copy(win.at[BACK, slot], zbuf.at[z, quad], load_sem.at[0])
    mine.start()
    mine.wait()
    arrived(0, zbuf.at[0, 0:3])

    @pl.loop(1, nz)
    def _(step):
        pltpu.make_async_remote_copy(
            src_ref=zbuf.at[z],
            dst_ref=zbuf.at[z],
            send_sem=send_sem.at[1],
            recv_sem=recv_sem.at[1],
            device_id=(ctx_of(quad, lax.rem(z + step, nz), nz), head),
            device_id_type=MESH,
        ).start()

    wanted = []
    for other in range(4):
        tile = tiles_ref[ctx_of(other, z, nz)]
        for back in range(BACK):
            wanted.append(jnp.maximum(tile - BACK + back, 0))

    def find(index, found):
        tile = tiles_ref[index]
        return tuple(jnp.where(tile == want, index, have) for want, have in zip(wanted, found))

    holders = lax.fori_loop(0, 4 * nz, find, tuple(jnp.int32(0) for _ in wanted))

    loads[2].wait()
    loads[3].wait()
    tile = tiles_ref[ctx_of(quad, z, nz)]
    base = (tile - BACK) * tile_rows
    high = lax.broadcasted_iota(jnp.int32, (1, rows), 1) // local_heads
    pos = tile * tile_rows + high
    low = jnp.zeros_like(pos)
    end = jnp.int32(0)
    for index in range(lengths_ref.shape[0]):
        end = end + lengths_ref[index]
        low = jnp.where(pos >= end, end, low)
    low_scr[...] = low - base
    at = lax.broadcasted_iota(jnp.int32, (tile_rows, rows), 0)

    def keys_of(block):
        return win[block, :, :, 0:width].reshape(tile_rows, width)

    def values_of(block):
        return win[block, :, :, width:width2].reshape(tile_rows, width)

    def scores(block, top):
        s = dot(keys_of(block), q_scr[...], ((1,), (1,)))
        live = at >= low_scr[...] - block * tile_rows
        if block == BACK:
            live = live & (at <= high)
        s = jnp.where(live, s, NEG_FILL)
        s_scr[block] = s
        return jnp.maximum(top, jnp.max(s.reshape(tile_rows // 8, 8, rows), axis=0))

    top = scores(BACK, jnp.full((8, rows), NEG_FILL, jnp.float32))
    cot_t[...] = c_scr[...].astype(jnp.float32).T
    dp_own[...] = dot(values_of(BACK), c_scr[...], ((1,), (1,)))

    arrived(1, zbuf.at[0 : nz - 1])

    for other in range(4):
        for back in range(BACK):
            holder = holders[other * BACK + back]
            from_z = lax.rem(lax.div(holder, 2), nz)
            from_quad = lax.div(holder, 2 * nz) * 2 + lax.rem(holder, 2)
            sbuf[other, back] = zbuf[from_z, from_quad]

    @pl.loop(1, slots)
    def _(step):
        other, other_quad, target = plane_target(step)
        pltpu.make_async_remote_copy(
            src_ref=sbuf.at[other_quad],
            dst_ref=win.at[0:BACK, slot],
            send_sem=send_sem.at[2],
            recv_sem=recv_sem.at[2],
            device_id=target,
            device_id_type=MESH,
        ).start()

    mine = pltpu.make_async_copy(sbuf.at[quad], win.at[0:BACK, slot], load_sem.at[0])
    mine.start()
    mine.wait()
    arrived(2, win.at[0:BACK, 0 : slots - 1])

    for block in range(BACK):
        top = scores(block, top)
    top = jnp.max(top, axis=0, keepdims=True) * log_scale
    total = jnp.zeros((8, rows), jnp.float32)
    out = jnp.zeros((width, rows), jnp.float32)
    for block in range(BACK + 1):
        p = jnp.exp2(s_scr[block] * log_scale - top)
        total = total + jnp.sum(p.reshape(tile_rows // 8, 8, rows), axis=0)
        p_low = p.astype(jnp.bfloat16)
        p_scr[block] = p_low
        out = out + dot(values_of(block), p_low, ((0,), (0,)))
    inverse = 1.0 / jnp.sum(total, axis=0, keepdims=True)
    out = (out * inverse).astype(jnp.bfloat16).astype(jnp.float32)
    att_scr[...] = out.T.astype(jnp.bfloat16)
    att_copy = pltpu.make_async_copy(att_scr, att_ref, load_sem.at[0])
    att_copy.start()
    cot = cot_t[...]
    delta = jnp.sum(cot * out, axis=0, keepdims=True) * inverse
    cot_scaled = cot * inverse
    cot_low = cot_scaled.astype(jnp.bfloat16)
    cot_rows = cot_scaled.T.astype(jnp.bfloat16)
    dq = jnp.zeros((width, rows), jnp.float32)
    for block in range(BACK + 1):
        p_low = p_scr[block]
        if block == BACK:
            dp = dp_own[...] * inverse
        else:
            dp = dot(values_of(block), cot_low, ((1,), (0,)))
        ds = (p_low.astype(jnp.float32) * (dp - delta)).astype(jnp.bfloat16)
        dv = dot(p_low, cot_rows, ((1,), (0,))).astype(jnp.bfloat16)
        dk = (dot(ds, q_scr[...], ((1,), (0,))) * scale).astype(jnp.bfloat16)
        terms[block, :, :, 0:width] = dk.reshape(slots, part, width)
        terms[block, :, :, width:width2] = dv.reshape(slots, part, width)
        dq = dq + dot(keys_of(block), ds, ((0,), (0,)))

    @pl.loop(1, slots)
    def _(step):
        other, other_quad, target = plane_target(step)
        pltpu.make_async_remote_copy(
            src_ref=terms.at[:, other],
            dst_ref=rbuf.at[slot],
            send_sem=send_sem.at[3],
            recv_sem=recv_sem.at[3],
            device_id=target,
            device_id_type=MESH,
        ).start()

    mine = pltpu.make_async_copy(terms.at[:, slot], rbuf.at[slot], load_sem.at[1])
    mine.start()
    dq_scr[...] = (dq * scale).T.astype(jnp.bfloat16)
    dq_copy = pltpu.make_async_copy(dq_scr, dq_ref, load_sem.at[2])
    dq_copy.start()
    mine.wait()
    arrived(3, rbuf.at[0 : slots - 1])

    for other in range(4):
        for back in range(BACK + 1):
            summed = rbuf[other * heads, back].astype(jnp.float32)
            for index in range(1, heads):
                summed = summed + rbuf[other * heads + index, back].astype(jnp.float32)
            acc[other, back] = summed

    sources = [tiles_ref[ctx_of(other, z, nz)] - BACK for other in range(4)]

    @pl.loop(0, nz)
    def _(step):
        to_z = lax.rem(z + step, nz)
        for to_quad in range(4):
            to_tile = tiles_ref[ctx_of(to_quad, to_z, nz)]
            summed = None
            for other in range(4):
                back = to_tile - sources[other]
                inside = jnp.logical_and(back >= 0, back <= BACK)
                loaded = acc[other, jnp.clip(back, 0, BACK)]
                term = jnp.where(inside, loaded, 0.0)
                summed = term if summed is None else summed + term
            zsend[to_z, to_quad] = summed.astype(zsend.dtype)

    @pl.loop(1, nz)
    def _(step):
        to_z = lax.rem(z + step, nz)
        pltpu.make_async_remote_copy(
            src_ref=zsend.at[to_z],
            dst_ref=zrecv.at[z],
            send_sem=send_sem.at[4],
            recv_sem=recv_sem.at[4],
            device_id=(ctx_of(quad, to_z, nz), head),
            device_id_type=MESH,
        ).start()

    mine = pltpu.make_async_copy(zsend.at[z], zrecv.at[z], load_sem.at[1])
    mine.start()
    mine.wait()
    arrived(4, zrecv.at[0 : nz - 1])
    summed = zrecv[0].astype(jnp.float32)
    for index in range(1, nz):
        summed = summed + zrecv[index].astype(jnp.float32)
    res[...] = summed.astype(res.dtype)

    @pl.loop(1, slots)
    def _(step):
        other, other_quad, target = plane_target(step)
        pltpu.make_async_remote_copy(
            src_ref=res.at[other_quad],
            dst_ref=out_ref.at[slot],
            send_sem=send_sem.at[5],
            recv_sem=recv_sem.at[5],
            device_id=target,
            device_id_type=MESH,
        ).start()

    mine = pltpu.make_async_copy(res.at[quad], out_ref.at[slot], load_sem.at[1])
    mine.start()
    mine.wait()
    att_copy.wait()
    dq_copy.wait()
    arrived(5, out_ref.at[0 : slots - 1])


def on_device(ctx_count, heads, queries, keys, values, grad_out, lengths, tile_of):
    tile_rows, local_heads, width = queries.shape
    rows = tile_rows * local_heads
    nz = ctx_count // 4
    slots = 4 * heads
    part = tile_rows // slots
    block = (part, 2 * width)
    low = keys.dtype
    smem = pl.BlockSpec(memory_space=pltpu.SMEM)
    anywhere = pl.BlockSpec(memory_space=pl.ANY)
    flat = jax.ShapeDtypeStruct((rows, width), low)
    attended, query_grad, sums = pl.pallas_call(
        functools.partial(fused_kernel, nz, heads, local_heads),
        out_shape=(flat, flat, jax.ShapeDtypeStruct((slots,) + block, low)),
        in_specs=[smem, smem, anywhere, anywhere, anywhere, anywhere],
        out_specs=(anywhere, anywhere, pl.BlockSpec(memory_space=pltpu.VMEM)),
        scratch_shapes=[
            pltpu.VMEM((BACK + 1, slots) + block, low),
            pltpu.VMEM((rows, width), low),
            pltpu.VMEM((rows, width), low),
            pltpu.VMEM((nz, 4) + block, low),
            pltpu.VMEM((4, BACK) + block, low),
            pltpu.VMEM((BACK + 1, tile_rows, rows), jnp.float32),
            pltpu.VMEM((BACK + 1, tile_rows, rows), low),
            pltpu.VMEM((tile_rows, rows), jnp.float32),
            pltpu.VMEM((width, rows), jnp.float32),
            pltpu.VMEM((1, rows), jnp.int32),
            pltpu.VMEM((rows, width), low),
            pltpu.VMEM((rows, width), low),
            pltpu.VMEM((BACK + 1, slots) + block, low),
            pltpu.VMEM((slots, BACK + 1) + block, low),
            pltpu.VMEM((4, BACK + 1) + block, jnp.float32),
            pltpu.VMEM((nz, 4) + block, low),
            pltpu.VMEM((nz, 4) + block, low),
            pltpu.VMEM((4,) + block, low),
            pltpu.SemaphoreType.DMA((4,)),
            pltpu.SemaphoreType.DMA((6,)),
            pltpu.SemaphoreType.DMA((6,)),
        ],
        compiler_params=pltpu.CompilerParams(
            collective_id=0, has_side_effects=True, vmem_limit_bytes=48 * 1024 * 1024
        ),
        name="ring_free_attention",
    )(
        tile_of,
        lengths,
        keys.reshape(slots, part, width),
        values.reshape(slots, part, width),
        queries.reshape(rows, width),
        grad_out.reshape(rows, width),
    )
    sums = sums.reshape(tile_rows, 2 * width)
    return (
        attended.reshape(queries.shape),
        query_grad.reshape(queries.shape),
        sums[:, :width].astype(jnp.float32),
        sums[:, width:].astype(jnp.float32),
    )


def solution(mesh):
    return jax.shard_map(
        functools.partial(on_device, mesh.shape["ctx"], mesh.shape["head"]),
        mesh=mesh,
        in_specs=(
            P("ctx", "head", None),
            P("ctx", None),
            P("ctx", None),
            P("ctx", "head", None),
            P(),
            P(),
        ),
        out_specs=(P("ctx", "head", None), P("ctx", "head", None), P("ctx", None), P("ctx", None)),
        check_vma=False,
    )
```
